768 devices in a mesh: sample: 32 (over y, z_hi, core), slab: 24 (over z_lo, x).
Axes of the slice: x: 4, y: 8, z: 12 (z_hi: 2, z_lo: 6; z = z_hi * 6 + z_lo), core: 2. Of those that a mesh axis runs over, the one named last changes fastest.
Arguments:
- volumes: bfloat16 [32, 48, 16, 32, 128], P('sample', 'slab'), may hold values from -6 to 6
- kernel: bfloat16 [3, 3, 3, 128, 256], replicated, may hold values from -0.109375 to 0.109375
- cotangent: bfloat16 [32, 24, 8, 16, 256], P('sample', 'slab'), may hold values from -6 to 6
Outputs:
- activations: bfloat16 [32, 24, 8, 16, 256], P('sample', 'slab')
- input_grads: bfloat16 [32, 48, 16, 32, 128], P('sample', 'slab')
- weight_grad: float32 [3456, 256], P('slab', 'sample')
The draws below stay inside these ranges and needn't reach their ends.
All inputs are finite; a program needn't handle non-finite values.
Results may differ from the reference program's by a relative error of at most 0.0049.
Values may be sent and summed in bfloat16 or wider, within the bound.
No kernel may reach another device: no remote copies, remote signals or barrier semaphores. Data moves between devices by JAX's collectives and lax.ppermute only.
A program may use at most 32 MiB of HBM per device.

```python
import math
import jax
import jax.numpy as jnp
from jax import lax

IN_CH = 128
OUT_CH = 256
HEIGHT = 16
WIDTH = 32
SAMPLES = 32
DEPTH = 48


def raised(values, rng, source, target, parts, factor):
    def block_of(axis_at):
        return (jnp.arange(values.shape[axis_at]) // (values.shape[axis_at] // parts)).reshape((-1,) + (1,) * (values.ndim - 1 - axis_at))

    first = jax.random.permutation(rng, parts)[block_of(target)]
    second = (block_of(target) + parts // 2) % parts
    return jnp.where((block_of(source) == first) | (block_of(source) == second), factor * values, values)


def shard_levels(own_key, extent, split, least, high):
    def one(dim, shards_of):
        draws = jax.random.uniform(jax.random.fold_in(jax.random.fold_in(own_key, 6), dim), (shards_of,), jnp.float32, least / len(split), high / len(split))
        return jnp.repeat(jnp.exp(draws), extent[dim] // shards_of).reshape((-1,) + (1,) * (len(extent) - dim - 1))

    level = one(*split[0])
    for cut in split[1:]:
        level = level * one(*cut)
    return level


def centred(key, shape, deviation, most, split=(), held_as=jnp.bfloat16):
    array = jax.random.normal(key, shape, jnp.float32) * deviation
    if len(split) > 0:
        array = shard_levels(key, shape, split, -0.22, 0.18) * array
    return jnp.clip(array, min=-most, max=most).astype(held_as)


def noise_with(rng, extent, scale, bound, split, heavy, held_as=jnp.bfloat16):
    array = scale * jax.random.normal(rng, extent, jnp.float32)
    if split:
        array = array * shard_levels(rng, extent, split, -0.22, 0.18)
    return jnp.clip(raised(array, jax.random.fold_in(rng, 3), *heavy), -bound, bound).astype(held_as)


def setup_inputs(seed: int = 0) -> dict:
    keys = jax.random.split(jax.random.key(seed), 4)
    volumes = centred(keys[0], (SAMPLES, DEPTH, HEIGHT, WIDTH, IN_CH), 1.0, 6.0, ((0, 32), (1, 24)))
    kernel = centred(keys[1], (3, 3, 3, IN_CH, OUT_CH), (27 * IN_CH) ** -0.5, 0.109375)
    cotangent = noise_with(keys[2], (SAMPLES, DEPTH // 2, HEIGHT // 2, WIDTH // 2, OUT_CH), 1.0, 6.0, ((0, 32), (1, 24)), (0, 4, 32, 2.75))
    return dict(volumes=volumes, kernel=kernel, cotangent=cotangent)


def activate(values):
    return 0.3 * values + 0.7 * values * jax.nn.sigmoid(values)

def slope_of(values):
    sigmoid_val = jax.nn.sigmoid(values)
    return 0.3 + 0.7 * (sigmoid_val + values * sigmoid_val * (1.0 - sigmoid_val))

def extract_taps(padded, out_depth, out_rows, out_cols):
    leading = padded.shape[0]
    channels = padded.shape[4]
    tap_list = []
    for depth_tap in range(3):
        for row_tap in range(3):
            for col_tap in range(3):
                tap_list.append(lax.slice(padded, (0, depth_tap, row_tap, col_tap, 0), (leading, depth_tap + 2 * out_depth - 1, row_tap + 2 * out_rows - 1, col_tap + 2 * out_cols - 1, channels), (1, 2, 2, 2, 1)))
    return jnp.stack(tap_list, axis=4).reshape(-1, 27 * channels)

def fold_taps(source, dim_index, target_len):
    tap_low = lax.index_in_dim(source, 0, 4, keepdims=False)
    tap_mid = lax.index_in_dim(source, 1, 4, keepdims=False)
    tap_high = lax.index_in_dim(source, 2, 4, keepdims=False)
    span_len = tap_low.shape[dim_index]

    def widen(segment, pad_low, pad_high):
        widths_pad = [(0, 0)] * segment.ndim
        widths_pad[dim_index] = (pad_low, pad_high)
        return jnp.pad(segment, widths_pad)
    even_part = widen(tap_low, 0, 1) + widen(tap_high, 1, 0)
    odd_part = widen(tap_mid, 0, 1)
    paired = jnp.stack([even_part, odd_part], axis=dim_index + 1)
    new_shape = list(even_part.shape)
    new_shape[dim_index] = 2 * (span_len + 1)
    return lax.slice_in_dim(paired.reshape(new_shape), 0, target_len, axis=dim_index)

def spread_taps(patch_grad, out_depth, out_rows, out_cols, depth_len, height_len, width_len):
    channels = patch_grad.shape[1] // 27
    shaped = patch_grad.reshape(-1, out_depth, out_rows, out_cols, 3, 3, 3, channels)
    shaped = fold_taps(shaped, 1, depth_len)
    shaped = fold_taps(shaped, 2, height_len)
    return fold_taps(shaped, 3, width_len)

def reference(volumes, kernel, cotangent):
    weight_rows = kernel.reshape(27 * IN_CH, OUT_CH)
    out_depth = DEPTH // 2
    out_rows = HEIGHT // 2
    out_cols = WIDTH // 2

    def per_sample(running, inputs):
        sample_volume, sample_cot = inputs
        padded = jnp.pad(sample_volume[None], ((0, 0), (1, 0), (1, 1), (1, 1), (0, 0)))
        patches = extract_taps(padded, out_depth, out_rows, out_cols)
        pre_act = jnp.dot(patches, weight_rows, preferred_element_type=jnp.float32)
        activation = activate(pre_act).astype(jnp.bfloat16)
        out_grad = (sample_cot.reshape(-1, OUT_CH).astype(jnp.float32) * slope_of(pre_act)).astype(jnp.bfloat16)
        running = running + lax.dot_general(patches, out_grad, (((0,), (0,)), ((), ())), preferred_element_type=jnp.float32)
        patch_grad = lax.dot_general(out_grad, weight_rows, (((1,), (1,)), ((), ())), preferred_element_type=jnp.float32)
        full_grad = spread_taps(patch_grad, out_depth, out_rows, out_cols, DEPTH + 1, HEIGHT + 2, WIDTH + 2)
        input_grad = full_grad[0, 1:, 1:HEIGHT + 1, 1:WIDTH + 1].astype(jnp.bfloat16)
        return (running, (activation.reshape(out_depth, out_rows, out_cols, OUT_CH), input_grad))
    running, outputs = lax.scan(per_sample, jnp.zeros((27 * IN_CH, OUT_CH), jnp.float32), (volumes, cotangent))
    norm_factor = 1.0 / math.sqrt(SAMPLES * out_depth * out_rows * out_cols)
    return (outputs[0], outputs[1], running * norm_factor)
```

```python
import math

import jax
import jax.numpy as jnp
from jax import lax
from jax.sharding import Mesh, PartitionSpec as P

Y, ZH, CORE, ZL, X = 8, 2, 2, 6, 4
AXES = ("y", "zh", "core", "zl", "x")
SLAB = ("zl", "x")


def shifted(block, distance):
    devices = range(ZL * X)
    route = [(i - distance, i) for i in devices if i - distance in devices]
    return lax.ppermute(block, SLAB, route)


def activate(values):
    return 0.3 * values + 0.7 * values * jax.nn.sigmoid(values)


def slope_of(values):
    sigmoid_val = jax.nn.sigmoid(values)
    return 0.3 + 0.7 * (sigmoid_val + values * sigmoid_val * (1.0 - sigmoid_val))


def extract_taps(padded, out_depth, out_rows, out_cols):
    leading = padded.shape[0]
    channels = padded.shape[4]
    tap_list = []
    for depth_tap in range(3):
        for row_tap in range(3):
            for col_tap in range(3):
                tap_list.append(
                    lax.slice(
                        padded,
                        (0, depth_tap, row_tap, col_tap, 0),
                        (
                            leading,
                            depth_tap + 2 * out_depth - 1,
                            row_tap + 2 * out_rows - 1,
                            col_tap + 2 * out_cols - 1,
                            channels,
                        ),
                        (1, 2, 2, 2, 1),
                    )
                )
    return jnp.stack(tap_list, axis=4).reshape(-1, 27 * channels)


def fold_taps(source, dim_index, target_len):
    tap_low = lax.index_in_dim(source, 0, 4, keepdims=False)
    tap_mid = lax.index_in_dim(source, 1, 4, keepdims=False)
    tap_high = lax.index_in_dim(source, 2, 4, keepdims=False)
    span_len = tap_low.shape[dim_index]

    def widen(segment, pad_low, pad_high):
        widths_pad = [(0, 0)] * segment.ndim
        widths_pad[dim_index] = (pad_low, pad_high)
        return jnp.pad(segment, widths_pad)

    even_part = widen(tap_low, 0, 1) + widen(tap_high, 1, 0)
    odd_part = widen(tap_mid, 0, 1)
    paired = jnp.stack([even_part, odd_part], axis=dim_index + 1)
    new_shape = list(even_part.shape)
    new_shape[dim_index] = 2 * (span_len + 1)
    return lax.slice_in_dim(paired.reshape(new_shape), 0, target_len, axis=dim_index)


def exchange(block, axes):
    return lax.all_to_all(block, axes, 0, 0, tiled=True)


def total(parts):
    return jnp.sum(parts.astype(jnp.float32), axis=0)


def reduce_weights(patches, out_grad, out_chans):
    wanted = jnp.arange(out_chans).reshape(Y, ZH, CORE, -1).transpose(2, 0, 1, 3).reshape(-1)
    choose = (jnp.arange(out_chans)[:, None] == wanted[None, :]).astype(jnp.bfloat16)
    reordered = jnp.dot(out_grad, choose, preferred_element_type=jnp.float32).astype(jnp.bfloat16)
    grad = lax.dot_general(
        patches, reordered, (((0,), (0,)), ((), ())), preferred_element_type=jnp.float32
    ).astype(jnp.bfloat16)
    rows = grad.shape[0] // (ZL * X)
    half = out_chans // CORE
    grad = grad.reshape(ZL, X, rows, CORE, half).transpose(3, 1, 0, 2, 4)
    grad = total(exchange(grad, "core")[:CORE]).astype(jnp.bfloat16)
    grad = total(exchange(grad, "x")).astype(jnp.bfloat16)
    grad = grad.reshape(ZL * rows, half).T.reshape(Y, half // Y, ZL * rows)
    grad = total(exchange(grad, "y"))
    filters = half // Y // ZH
    grad = grad.reshape(ZH, filters, ZL, rows).transpose(0, 2, 1, 3).reshape(ZH * ZL, filters, rows)
    return total(exchange(grad, ("zh", "zl"))).T


def local(volumes, kernel, cotangent):
    batch_rows, slab_len, height_len, width_len, in_chans = volumes.shape
    out_chans = kernel.shape[-1]
    out_depth = slab_len // 2
    out_rows = height_len // 2
    out_cols = width_len // 2
    weight_rows = kernel.reshape(27 * in_chans, out_chans)
    below_layer = shifted(volumes[:, slab_len - 1 :], 1)
    extended = jnp.concatenate([below_layer, volumes], axis=1)
    padded = jnp.pad(extended, ((0, 0), (0, 0), (1, 1), (1, 1), (0, 0)))
    patches = extract_taps(padded, out_depth, out_rows, out_cols)
    pre_act = jnp.dot(patches, weight_rows, preferred_element_type=jnp.float32)
    activation = activate(pre_act).astype(jnp.bfloat16)
    out_grad = (cotangent.reshape(-1, out_chans).astype(jnp.float32) * slope_of(pre_act)).astype(
        jnp.bfloat16
    )
    patch_grad = lax.dot_general(
        out_grad, weight_rows, (((1,), (1,)), ((), ())), preferred_element_type=jnp.float32
    )
    shaped = patch_grad.reshape(batch_rows, out_depth, out_rows, out_cols, 3, 3, 3, in_chans)
    shaped = fold_taps(shaped, 1, slab_len + 1)
    shaped = fold_taps(shaped, 2, height_len + 2)
    full_grad = fold_taps(shaped, 3, width_len + 2)
    interior = full_grad[:, 1:, 1 : height_len + 1, 1 : width_len + 1]
    rim_layer = full_grad[:, 0:1, 1 : height_len + 1, 1 : width_len + 1]
    from_next = shifted(rim_layer, -1)
    input_grad = jnp.concatenate(
        [interior[:, : slab_len - 1], interior[:, slab_len - 1 :] + from_next], axis=1
    ).astype(jnp.bfloat16)
    grad_shard = reduce_weights(patches, out_grad, out_chans)
    total_cells = Y * ZH * CORE * batch_rows * ZL * X * out_depth * out_rows * out_cols
    norm_factor = 1.0 / math.sqrt(total_cells)
    activations = activation.reshape(batch_rows, out_depth, out_rows, out_cols, out_chans)
    return (activations, input_grad, grad_shard * norm_factor)


def solution(mesh):
    fine = Mesh(mesh.devices.reshape(Y, ZH, CORE, ZL, X), AXES)
    split = P(("y", "zh", "core"), SLAB, None, None, None)
    out_specs = (split, split, P(SLAB, ("y", "zh", "core")))
    return jax.shard_map(local, mesh=fine, in_specs=(split, P(), split), out_specs=out_specs, check_vma=False)
```

```python
import math

import jax
import jax.numpy as jnp
from jax import lax
from jax.experimental import pallas as pl
from jax.experimental.pallas import tpu as pltpu
from jax.sharding import Mesh, PartitionSpec as P

Y, ZH, CORE, ZL, X = 8, 2, 2, 6, 4
AXES = ("y", "zh", "core", "zl", "x")
SLAB = ("zl", "x")
ROWS, COLS = 8, 16
IN, OUT = 128, 256
CELLS = ROWS * COLS
TAPS = [(a, b, c) for a in range(3) for b in range(3) for c in range(3)]
SHARE = 27 * IN // (ZL * X)
HALF = OUT // CORE
PAD = 8
BF, F32 = jnp.bfloat16, jnp.float32
VMEM = pl.BlockSpec(memory_space=pltpu.VMEM)


def shifted(block, distance):
    devices = range(ZL * X)
    route = [(i - distance, i) for i in devices if i - distance in devices]
    return lax.ppermute(block, SLAB, route)


def forward_kernel(own_ref, below_ref, weight_ref, cot_ref, act_ref, grad_ref, dw_ref, wide, patches):
    zero = jnp.zeros((COLS, IN), BF)
    for layer in range(3):
        for h in range(2 * ROWS):
            source = below_ref[h] if layer == 0 else own_ref[layer - 1, h]
            wide[layer, h, 0:PAD, :] = jnp.zeros((PAD, IN), F32)
            wide[layer, h, PAD : PAD + 2 * COLS, :] = source.astype(F32)
    for tap, (a, b, c) in enumerate(TAPS):
        lanes = slice(tap * IN, (tap + 1) * IN)
        for p in range(ROWS):
            h = 2 * p - 1 + b
            if h < 0:
                piece = zero
            else:
                piece = wide[a, h, pl.ds(PAD - 1 + c, COLS, stride=2), :].astype(BF)
            patches[p * COLS : (p + 1) * COLS, lanes] = piece
    pre = jnp.dot(patches[...], weight_ref[...], preferred_element_type=F32)
    sig = jax.nn.sigmoid(pre)
    act_ref[...] = (0.3 * pre + 0.7 * pre * sig).astype(BF)
    slope = 0.3 + 0.7 * (sig + pre * sig * (1.0 - sig))
    grad = (cot_ref[...].astype(F32) * slope).astype(BF)
    grad_ref[...] = grad
    place = lax.broadcasted_iota(jnp.int32, (OUT, OUT), 1)
    origin = lax.broadcasted_iota(jnp.int32, (OUT, OUT), 0)
    wanted = (place % HALF) // 8 * 16 + place // HALF * 8 + place % 8
    choose = jnp.where(origin == wanted, 1.0, 0.0).astype(BF)
    ordered = jnp.dot(grad, choose, preferred_element_type=F32).astype(BF)
    for tap in range(27):
        lanes = slice(tap * IN, (tap + 1) * IN)
        part = lax.dot_general(
            patches[:, lanes], ordered, (((0,), (0,)), ((), ())), preferred_element_type=F32
        ).astype(BF)
        for k in range(IN // 16):
            slab, inner = divmod(tap * (IN // 16) + k, SHARE // 16)
            zl, x = divmod(slab, X)
            for core in range(CORE):
                dw_ref[core, x, zl, inner * 16 : (inner + 1) * 16, :] = part[
                    k * 16 : (k + 1) * 16, core * HALF : (core + 1) * HALF
                ]


def forward(own, below, weights, cotangent):
    return pl.pallas_call(
        forward_kernel,
        out_shape=(
            jax.ShapeDtypeStruct((CELLS, OUT), BF),
            jax.ShapeDtypeStruct((CELLS, OUT), BF),
            jax.ShapeDtypeStruct((CORE, X, ZL, SHARE, HALF), BF),
        ),
        in_specs=[VMEM] * 4,
        out_specs=(VMEM,) * 3,
        scratch_shapes=[
            pltpu.VMEM((3, 2 * ROWS, PAD + 2 * COLS, IN), F32),
            pltpu.VMEM((CELLS, 27 * IN), BF),
        ],
        cost_estimate=pl.CostEstimate(flops=4 * CELLS * 27 * IN * OUT, bytes_accessed=4 << 20, transcendentals=CELLS * OUT),
        name="forward",
    )(own, below, weights, cotangent)


def backward_kernel(grad_ref, next_ref, weight_ref, out_ref, wide):
    def moved(ref):
        grad = ref[...].astype(F32)
        cell = lax.broadcasted_iota(jnp.int32, (CELLS, OUT), 0)
        ahead = jnp.concatenate([grad[1:], jnp.zeros((1, OUT), F32)], axis=0)
        ahead = jnp.where(cell % COLS == COLS - 1, 0.0, ahead)
        blank = jnp.zeros((COLS, OUT), BF)
        found = {}
        for dq, value in ((0, ref[...]), (1, ahead.astype(BF))):
            found[0, dq] = value
            found[1, dq] = jnp.concatenate([value[COLS:], blank], axis=0)
        return found

    mine, after = moved(grad_ref), moved(next_ref)
    choices = {0: [(1, 0)], 1: [(2, 0), (0, 1)]}
    for layer in range(2):
        sources = [(1, mine)] if layer == 0 else [(2, mine), (0, after)]
        for hp in range(2):
            for wp in range(2):
                value = jnp.zeros((CELLS, IN), F32)
                for a, found in sources:
                    for b, dp in choices[hp]:
                        for c, dq in choices[wp]:
                            value += lax.dot_general(
                                found[dp, dq],
                                weight_ref[(a * 3 + b) * 3 + c],
                                (((1,), (1,)), ((), ())),
                                preferred_element_type=F32,
                            )
                for p in range(ROWS):
                    wide[layer, 2 * p + hp, pl.ds(wp, COLS, stride=2), :] = value[p * COLS : (p + 1) * COLS]
    out_ref[...] = wide[...].astype(BF)


def backward(grad, grad_next, weights):
    return pl.pallas_call(
        backward_kernel,
        out_shape=jax.ShapeDtypeStruct((2, 2 * ROWS, 2 * COLS, IN), BF),
        in_specs=[VMEM] * 3,
        out_specs=VMEM,
        scratch_shapes=[pltpu.VMEM((2, 2 * ROWS, 2 * COLS, IN), F32)],
        cost_estimate=pl.CostEstimate(flops=2 * CELLS * 27 * IN * OUT, bytes_accessed=3 << 20, transcendentals=0),
        name="backward",
    )(grad, grad_next, weights)


def exchange(block, axes):
    return lax.all_to_all(block, axes, 0, 0, tiled=True)


def total(parts):
    return jnp.sum(parts.astype(F32), axis=0)


def reduce_weights(grad):
    grad = total(exchange(grad, "core")).astype(BF)
    grad = total(exchange(grad, "x")).astype(BF)
    grad = grad.reshape(ZL * SHARE, HALF).T.reshape(Y, HALF // Y, ZL * SHARE)
    grad = total(exchange(grad, "y"))
    grad = grad.reshape(ZH, 8, ZL, SHARE).transpose(0, 2, 1, 3).reshape(ZH * ZL, 8, SHARE)
    return total(exchange(grad, ("zh", "zl"))).T


def local(volumes, kernel, cotangent):
    own = volumes[0]
    below = shifted(volumes[0, 1], 1)
    activation, out_grad, partial = forward(
        own, below, kernel.reshape(27 * IN, OUT), cotangent.reshape(CELLS, OUT)
    )
    next_grad = shifted(out_grad, -1)
    input_grad = backward(out_grad, next_grad, kernel.reshape(27, IN, OUT))
    grad_shard = reduce_weights(partial)
    norm_factor = 1.0 / math.sqrt(Y * ZH * CORE * ZL * X * CELLS)
    return (
        activation.reshape(1, 1, ROWS, COLS, OUT),
        input_grad[None],
        grad_shard * norm_factor,
    )


def solution(mesh):
    fine = Mesh(mesh.devices.reshape(Y, ZH, CORE, ZL, X), AXES)
    split = P(("y", "zh", "core"), SLAB, None, None, None)
    out_specs = (split, split, P(SLAB, ("y", "zh", "core")))
    return jax.shard_map(local, mesh=fine, in_specs=(split, P(), split), out_specs=out_specs, check_vma=False)
```

```python
import math

import jax
import jax.numpy as jnp
from jax import lax
from jax.experimental import pallas as pl
from jax.experimental.pallas import tpu as pltpu
from jax.sharding import Mesh, PartitionSpec as P


Y, ZH, CORE, ZL, X = 8, 2, 2, 6, 4
AXES = ("y", "zh", "core", "zl", "x")
SLAB = ("zl", "x")
ROWS, COLS = 8, 16
IN, OUT = 128, 256
CELLS = ROWS * COLS
SHARE = 27 * IN // (ZL * X)
HALF = OUT // CORE
PAD = 8
GRANT = 12 << 20
BF, F32 = jnp.bfloat16, jnp.float32
VMEM = pl.BlockSpec(memory_space=pltpu.VMEM)


def shifted(block, distance):
    devices = range(ZL * X)
    route = [(i - distance, i) for i in devices if i - distance in devices]
    return lax.ppermute(block, SLAB, route)


def widen(wide, layer, h, source):
    wide[layer, h, 0:PAD, :] = jnp.zeros((PAD, IN), F32)
    wide[layer, h, PAD : PAD + 2 * COLS, :] = source.astype(F32)


def fill_patches(wide, layer, patches, first):
    for b in range(3):
        for c in range(3):
            lanes = slice((first + b * 3 + c) * IN, (first + b * 3 + c + 1) * IN)
            for p in range(ROWS):
                h = 2 * p - 1 + b
                if h < 0:
                    piece = jnp.zeros((COLS, IN), BF)
                else:
                    piece = wide[layer, h, pl.ds(PAD - 1 + c, COLS, stride=2), :].astype(BF)
                patches[p * COLS : (p + 1) * COLS, lanes] = piece


def own_kernel(low_ref, high_ref, weight_hbm, patches, pre_ref, weight_ref, wide, sem):
    copy = pltpu.make_async_copy(weight_hbm, weight_ref, sem)
    copy.start()
    for layer, source in enumerate((low_ref, high_ref)):
        for h in range(2 * ROWS):
            widen(wide, layer, h, source[h])
        fill_patches(wide, layer, patches, 9 * layer)
    copy.wait()
    pre_ref[...] = jnp.dot(patches[...], weight_ref[9 * IN :, :], preferred_element_type=F32)


def own_taps(low, high, weights):
    return pl.pallas_call(
        own_kernel,
        out_shape=(
            jax.ShapeDtypeStruct((CELLS, 18 * IN), BF),
            jax.ShapeDtypeStruct((CELLS, OUT), F32),
            jax.ShapeDtypeStruct((27 * IN, OUT), BF),
        ),
        in_specs=[VMEM] * 2 + [pl.BlockSpec(memory_space=pltpu.HBM)],
        out_specs=(VMEM,) * 3,
        scratch_shapes=[
            pltpu.VMEM((2, 2 * ROWS, PAD + 2 * COLS, IN), F32),
            pltpu.SemaphoreType.DMA(()),
        ],
        cost_estimate=pl.CostEstimate(flops=2 * CELLS * 18 * IN * OUT, bytes_accessed=3 << 20, transcendentals=0),
        compiler_params=pltpu.CompilerParams(vmem_limit_bytes=GRANT),
        name="own_taps",
    )(low, high, weights)


def weight_terms(patches, first, tap, grad, keep_ref, send_ref):
    lanes = slice((tap - first) * IN, (tap - first + 1) * IN)
    part = lax.dot_general(
        patches[:, lanes], grad, (((0,), (0,)), ((), ())), preferred_element_type=F32
    ).astype(BF)
    for k in range(IN // 16):
        slab, inner = divmod(tap * (IN // 16) + k, SHARE // 16)
        zl, x = divmod(slab, X)
        for half, ref in enumerate((keep_ref, send_ref)):
            ref[x, zl, inner * 16 : (inner + 1) * 16, :] = part[
                k * 16 : (k + 1) * 16, half * HALF : (half + 1) * HALF
            ]


def forward_kernel(
    me_ref, below_ref, weight_ref, own_patches, pre_ref, cot_ref, act_ref, grad_ref, keep_ref, send_ref, patches, wide
):
    for h in range(2 * ROWS):
        widen(wide, 0, h, below_ref[h])
    fill_patches(wide, 0, patches, 0)
    pre = pre_ref[...] + jnp.dot(patches[...], weight_ref[: 9 * IN, :], preferred_element_type=F32)
    sig = jax.nn.sigmoid(pre)
    act_ref[...] = (0.3 * pre + 0.7 * pre * sig).astype(BF)
    slope = 0.3 + 0.7 * (sig + pre * sig * (1.0 - sig))
    grad = (cot_ref[...].astype(F32) * slope).astype(BF)
    grad_ref[...] = grad
    me = me_ref[0]
    place = lax.broadcasted_iota(jnp.int32, (OUT, OUT), 1)
    origin = lax.broadcasted_iota(jnp.int32, (OUT, OUT), 0)
    who = jnp.where(place < HALF, me, 1 - me)
    wanted = (place % HALF) // 8 * 16 + who * 8 + place % 8
    choose = jnp.where(origin == wanted, 1.0, 0.0).astype(BF)
    ordered = jnp.dot(grad, choose, preferred_element_type=F32).astype(BF)
    for tap in range(27):
        held, first = (patches, 0) if tap < 9 else (own_patches, 9)
        weight_terms(held, first, tap, ordered, keep_ref, send_ref)


def forward(me, below, weights, own_patches, pre, cotangent):
    return pl.pallas_call(
        forward_kernel,
        out_shape=(
            jax.ShapeDtypeStruct((CELLS, OUT), BF),
            jax.ShapeDtypeStruct((CELLS, OUT), BF),
            jax.ShapeDtypeStruct((X, ZL, SHARE, HALF), BF),
            jax.ShapeDtypeStruct((X, ZL, SHARE, HALF), BF),
        ),
        in_specs=[pl.BlockSpec(memory_space=pltpu.SMEM)] + [VMEM] * 5,
        out_specs=(VMEM,) * 4,
        scratch_shapes=[
            pltpu.VMEM((CELLS, 9 * IN), BF),
            pltpu.VMEM((1, 2 * ROWS, PAD + 2 * COLS, IN), F32),
        ],
        cost_estimate=pl.CostEstimate(flops=3 * CELLS * 27 * IN * OUT, bytes_accessed=3 << 20, transcendentals=CELLS * OUT),
        compiler_params=pltpu.CompilerParams(vmem_limit_bytes=GRANT),
        name="forward",
    )(me, below, weights, own_patches, pre, cotangent)


def backward_kernel(grad_ref, next_ref, weight_ref, out_ref, wide):
    def moved(ref):
        grad = ref[...].astype(F32)
        cell = lax.broadcasted_iota(jnp.int32, (CELLS, OUT), 0)
        ahead = jnp.concatenate([grad[1:], jnp.zeros((1, OUT), F32)], axis=0)
        ahead = jnp.where(cell % COLS == COLS - 1, 0.0, ahead)
        blank = jnp.zeros((COLS, OUT), BF)
        found = {}
        for dq, value in ((0, ref[...]), (1, ahead.astype(BF))):
            found[0, dq] = value
            found[1, dq] = jnp.concatenate([value[COLS:], blank], axis=0)
        return found

    mine, after = moved(grad_ref), moved(next_ref)
    choices = {0: [(1, 0)], 1: [(2, 0), (0, 1)]}
    for layer in range(2):
        sources = [(1, mine)] if layer == 0 else [(2, mine), (0, after)]
        for hp in range(2):
            for wp in range(2):
                value = jnp.zeros((CELLS, IN), F32)
                for a, found in sources:
                    for b, dp in choices[hp]:
                        for c, dq in choices[wp]:
                            value += lax.dot_general(
                                found[dp, dq],
                                weight_ref[(a * 3 + b) * 3 + c],
                                (((1,), (1,)), ((), ())),
                                preferred_element_type=F32,
                            )
                for p in range(ROWS):
                    wide[layer, 2 * p + hp, pl.ds(wp, COLS, stride=2), :] = value[p * COLS : (p + 1) * COLS]
    out_ref[...] = wide[...].astype(BF)


def backward(grad, grad_next, weights):
    return pl.pallas_call(
        backward_kernel,
        out_shape=jax.ShapeDtypeStruct((2, 2 * ROWS, 2 * COLS, IN), BF),
        in_specs=[VMEM] * 3,
        out_specs=VMEM,
        scratch_shapes=[pltpu.VMEM((2, 2 * ROWS, 2 * COLS, IN), F32)],
        cost_estimate=pl.CostEstimate(flops=2 * CELLS * 27 * IN * OUT, bytes_accessed=3 << 20, transcendentals=0),
        compiler_params=pltpu.CompilerParams(vmem_limit_bytes=GRANT),
        name="backward",
    )(grad, grad_next, weights)


def exchange(block, axes):
    return lax.all_to_all(block, axes, 0, 0, tiled=True)


def total(parts):
    return jnp.sum(parts.astype(F32), axis=0)


def local(volumes, kernel, cotangent):
    low, high = volumes[0, 0], volumes[0, 1]
    below = shifted(high, 1)
    own_patches, pre, weights = own_taps(low, high, kernel.reshape(27 * IN, OUT))
    me = lax.axis_index("core").reshape(1)
    activation, out_grad, keep, send = forward(
        me, below, weights, own_patches, pre, cotangent.reshape(CELLS, OUT)
    )
    partner = lax.ppermute(send, "core", [(0, 1), (1, 0)])
    next_grad = shifted(out_grad, -1)
    grad = (keep.astype(F32) + partner.astype(F32)).astype(BF)
    grad = exchange(grad, "x")
    grad, out_grad = lax.optimization_barrier((grad, out_grad))
    input_grad = backward(out_grad, next_grad, weights.reshape(27, IN, OUT))
    grad, input_grad = lax.optimization_barrier((grad, input_grad))
    grad = total(grad).astype(BF)
    grad = grad.reshape(ZL * SHARE, HALF).T.reshape(Y, HALF // Y, ZL * SHARE)
    grad = total(exchange(grad, "y"))
    grad = grad.reshape(ZH, 8, ZL, SHARE).transpose(0, 2, 1, 3).reshape(ZH * ZL, 8, SHARE)
    grad = total(exchange(grad, ("zh", "zl"))).T
    norm_factor = 1.0 / math.sqrt(Y * ZH * CORE * ZL * X * CELLS)
    return (
        activation.reshape(1, 1, ROWS, COLS, OUT),
        input_grad[None],
        grad * norm_factor,
    )


def solution(mesh):
    fine = Mesh(mesh.devices.reshape(Y, ZH, CORE, ZL, X), AXES)
    split = P(("y", "zh", "core"), SLAB, None, None, None)
    out_specs = (split, split, P(SLAB, ("y", "zh", "core")))
    return jax.shard_map(local, mesh=fine, in_specs=(split, P(), split), out_specs=out_specs, check_vma=False)
```

```python
import math

import jax
import jax.numpy as jnp
from jax import lax
from jax.experimental import pallas as pl
from jax.experimental.pallas import tpu as pltpu
from jax.sharding import Mesh, PartitionSpec as P


Y, ZH, CORE, ZL, X = 8, 2, 2, 6, 4
AXES = ("y", "zh", "core", "zl", "x")
SLAB = ("zl", "x")
ROWS, COLS = 8, 16
IN, OUT = 128, 256
CELLS = ROWS * COLS
SHARE = 27 * IN // (ZL * X)
HALF = OUT // CORE
PAD = 8
GRANT = 12 << 20
BF, F32 = jnp.bfloat16, jnp.float32
VMEM = pl.BlockSpec(memory_space=pltpu.VMEM)


def shifted(block, distance):
    devices = range(ZL * X)
    route = [(i - distance, i) for i in devices if i - distance in devices]
    return lax.ppermute(block, SLAB, route)


def widen(wide, layer, h, source):
    wide[layer, h, 0:PAD, :] = jnp.zeros((PAD, IN), F32)
    wide[layer, h, PAD : PAD + 2 * COLS, :] = source.astype(F32)


def fill_patches(wide, layer, patches, first):
    for b in range(3):
        for c in range(3):
            lanes = slice((first + b * 3 + c) * IN, (first + b * 3 + c + 1) * IN)
            for p in range(ROWS):
                h = 2 * p - 1 + b
                if h < 0:
                    piece = jnp.zeros((COLS, IN), BF)
                else:
                    piece = wide[layer, h, pl.ds(PAD - 1 + c, COLS, stride=2), :].astype(BF)
                patches[p * COLS : (p + 1) * COLS, lanes] = piece


def own_kernel(low_ref, high_ref, weight_hbm, patches, pre_ref, weight_ref, wide, sem):
    copy = pltpu.make_async_copy(weight_hbm, weight_ref, sem)
    copy.start()
    for layer, source in enumerate((low_ref, high_ref)):
        for h in range(2 * ROWS):
            widen(wide, layer, h, source[h])
        fill_patches(wide, layer, patches, 9 * layer)
    copy.wait()
    pre_ref[...] = jnp.dot(patches[...], weight_ref[9 * IN :, :], preferred_element_type=F32)


def own_taps(low, high, weights):
    return pl.pallas_call(
        own_kernel,
        out_shape=(
            jax.ShapeDtypeStruct((CELLS, 18 * IN), BF),
            jax.ShapeDtypeStruct((CELLS, OUT), F32),
            jax.ShapeDtypeStruct((27 * IN, OUT), BF),
        ),
        in_specs=[VMEM] * 2 + [pl.BlockSpec(memory_space=pltpu.HBM)],
        out_specs=(VMEM,) * 3,
        scratch_shapes=[
            pltpu.VMEM((2, 2 * ROWS, PAD + 2 * COLS, IN), F32),
            pltpu.SemaphoreType.DMA(()),
        ],
        cost_estimate=pl.CostEstimate(flops=2 * CELLS * 18 * IN * OUT, bytes_accessed=3 << 20, transcendentals=0),
        compiler_params=pltpu.CompilerParams(vmem_limit_bytes=GRANT),
        name="own_taps",
    )(low, high, weights)


def weight_terms(patches, first, tap, grad, keep_ref, send_ref):
    lanes = slice((tap - first) * IN, (tap - first + 1) * IN)
    part = lax.dot_general(
        patches[:, lanes], grad, (((0,), (0,)), ((), ())), preferred_element_type=F32
    ).astype(BF)
    for k in range(IN // 16):
        slab, inner = divmod(tap * (IN // 16) + k, SHARE // 16)
        zl, x = divmod(slab, X)
        for half, ref in enumerate((keep_ref, send_ref)):
            ref[x, zl, inner * 16 : (inner + 1) * 16, :] = part[
                k * 16 : (k + 1) * 16, half * HALF : (half + 1) * HALF
            ]


def forward_kernel(
    me_ref, below_ref, weight_ref, own_patches, pre_ref, cot_ref, act_ref, grad_ref, keep_ref, send_ref, patches, wide
):
    for h in range(2 * ROWS):
        widen(wide, 0, h, below_ref[h])
    fill_patches(wide, 0, patches, 0)
    pre = pre_ref[...] + jnp.dot(patches[...], weight_ref[: 9 * IN, :], preferred_element_type=F32)
    sig = jax.nn.sigmoid(pre)
    act_ref[...] = (0.3 * pre + 0.7 * pre * sig).astype(BF)
    slope = 0.3 + 0.7 * (sig + pre * sig * (1.0 - sig))
    grad = (cot_ref[...].astype(F32) * slope).astype(BF)
    grad_ref[...] = grad
    me = me_ref[0]
    place = lax.broadcasted_iota(jnp.int32, (OUT, OUT), 1)
    origin = lax.broadcasted_iota(jnp.int32, (OUT, OUT), 0)
    who = jnp.where(place < HALF, me, 1 - me)
    wanted = (place % HALF) // 8 * 16 + who * 8 + place % 8
    choose = jnp.where(origin == wanted, 1.0, 0.0).astype(BF)
    ordered = jnp.dot(grad, choose, preferred_element_type=F32).astype(BF)
    for tap in range(27):
        held, first = (patches, 0) if tap < 9 else (own_patches, 9)
        weight_terms(held, first, tap, ordered, keep_ref, send_ref)


def forward(me, below, weights, own_patches, pre, cotangent):
    return pl.pallas_call(
        forward_kernel,
        out_shape=(
            jax.ShapeDtypeStruct((CELLS, OUT), BF),
            jax.ShapeDtypeStruct((CELLS, OUT), BF),
            jax.ShapeDtypeStruct((X, ZL, SHARE, HALF), BF),
            jax.ShapeDtypeStruct((X, ZL, SHARE, HALF), BF),
        ),
        in_specs=[pl.BlockSpec(memory_space=pltpu.SMEM)] + [VMEM] * 5,
        out_specs=(VMEM,) * 4,
        scratch_shapes=[
            pltpu.VMEM((CELLS, 9 * IN), BF),
            pltpu.VMEM((1, 2 * ROWS, PAD + 2 * COLS, IN), F32),
        ],
        cost_estimate=pl.CostEstimate(flops=3 * CELLS * 27 * IN * OUT, bytes_accessed=3 << 20, transcendentals=CELLS * OUT),
        compiler_params=pltpu.CompilerParams(vmem_limit_bytes=GRANT),
        name="forward",
    )(me, below, weights, own_patches, pre, cotangent)


def backward_kernel(grad_ref, next_ref, weight_ref, out_ref, wide):
    def moved(ref):
        grad = ref[...].astype(F32)
        cell = lax.broadcasted_iota(jnp.int32, (CELLS, OUT), 0)
        ahead = jnp.concatenate([grad[1:], jnp.zeros((1, OUT), F32)], axis=0)
        ahead = jnp.where(cell % COLS == COLS - 1, 0.0, ahead)
        blank = jnp.zeros((COLS, OUT), BF)
        found = {}
        for dq, value in ((0, ref[...]), (1, ahead.astype(BF))):
            found[0, dq] = value
            found[1, dq] = jnp.concatenate([value[COLS:], blank], axis=0)
        return found

    mine, after = moved(grad_ref), moved(next_ref)
    choices = {0: [(1, 0)], 1: [(2, 0), (0, 1)]}
    for layer in range(2):
        sources = [(1, mine)] if layer == 0 else [(2, mine), (0, after)]
        for hp in range(2):
            for wp in range(2):
                value = jnp.zeros((CELLS, IN), F32)
                for a, found in sources:
                    for b, dp in choices[hp]:
                        for c, dq in choices[wp]:
                            value += lax.dot_general(
                                found[dp, dq],
                                weight_ref[(a * 3 + b) * 3 + c],
                                (((1,), (1,)), ((), ())),
                                preferred_element_type=F32,
                            )
                for p in range(ROWS):
                    wide[layer, 2 * p + hp, pl.ds(wp, COLS, stride=2), :] = value[p * COLS : (p + 1) * COLS]
    out_ref[...] = wide[...].astype(BF)


def backward(grad, grad_next, weights):
    return pl.pallas_call(
        backward_kernel,
        out_shape=jax.ShapeDtypeStruct((2, 2 * ROWS, 2 * COLS, IN), BF),
        in_specs=[VMEM] * 3,
        out_specs=VMEM,
        scratch_shapes=[pltpu.VMEM((2, 2 * ROWS, 2 * COLS, IN), F32)],
        cost_estimate=pl.CostEstimate(flops=2 * CELLS * 27 * IN * OUT, bytes_accessed=3 << 20, transcendentals=0),
        compiler_params=pltpu.CompilerParams(vmem_limit_bytes=GRANT),
        name="backward",
    )(grad, grad_next, weights)


def exchange(block, axes):
    return lax.all_to_all(block, axes, 0, 0, tiled=True)


def total(parts):
    return jnp.sum(parts.astype(F32), axis=0)


def local(volumes, kernel, cotangent):
    low, high = volumes[0, 0], volumes[0, 1]
    below = shifted(high, 1)
    own_patches, pre, weights = own_taps(low, high, kernel.reshape(27 * IN, OUT))
    me = lax.axis_index("core").reshape(1)
    activation, out_grad, keep, send = forward(
        me, below, weights, own_patches, pre, cotangent.reshape(CELLS, OUT)
    )
    partner = lax.ppermute(send, "core", [(0, 1), (1, 0)])
    next_grad = shifted(out_grad, -1)
    grad = (keep.astype(F32) + partner.astype(F32)).astype(BF)
    grad = exchange(grad, "x")
    grad = total(grad).astype(BF)
    grad = grad.reshape(ZL * SHARE, HALF).T.reshape(Y, HALF // Y, ZL * SHARE)
    grad, out_grad = lax.optimization_barrier((exchange(grad, "y"), out_grad))
    input_grad = backward(out_grad, next_grad, weights.reshape(27, IN, OUT))
    grad = total(grad)
    grad = grad.reshape(ZH, 8, ZL, SHARE).transpose(0, 2, 1, 3).reshape(ZH * ZL, 8, SHARE)
    grad = total(exchange(grad, ("zh", "zl"))).T
    norm_factor = 1.0 / math.sqrt(Y * ZH * CORE * ZL * X * CELLS)
    return (
        activation.reshape(1, 1, ROWS, COLS, OUT),
        input_grad[None],
        grad * norm_factor,
    )


def solution(mesh):
    fine = Mesh(mesh.devices.reshape(Y, ZH, CORE, ZL, X), AXES)
    split = P(("y", "zh", "core"), SLAB, None, None, None)
    out_specs = (split, split, P(SLAB, ("y", "zh", "core")))
    return jax.shard_map(local, mesh=fine, in_specs=(split, P(), split), out_specs=out_specs, check_vma=False)
```

```python
import math

import jax
import jax.numpy as jnp
from jax import lax
from jax.experimental import pallas as pl
from jax.experimental.pallas import tpu as pltpu
from jax.sharding import Mesh, PartitionSpec as P


Y, ZH, CORE, ZQ, ZP, X = 8, 2, 2, 3, 2, 4
ZL = ZQ * ZP
AXES = ("y", "zh", "core", "zq", "zp", "x")
SLAB = ("zq", "zp", "x")
ROWS, COLS = 8, 16
IN, OUT = 128, 256
CELLS = ROWS * COLS
SHARE = 27 * IN // (ZL * X)
HALF = OUT // CORE
PAD = 8
GRANT = 12 << 20
BF, F32 = jnp.bfloat16, jnp.float32
VMEM = pl.BlockSpec(memory_space=pltpu.VMEM)


def shifted(block, distance):
    devices = range(ZL * X)
    route = [(i - distance, i) for i in devices if i - distance in devices]
    return lax.ppermute(block, SLAB, route)


def widen(wide, layer, h, source):
    wide[layer, h, 0:PAD, :] = jnp.zeros((PAD, IN), F32)
    wide[layer, h, PAD : PAD + 2 * COLS, :] = source.astype(F32)


def fill_patches(wide, layer, patches, first):
    for b in range(3):
        for c in range(3):
            lanes = slice((first + b * 3 + c) * IN, (first + b * 3 + c + 1) * IN)
            for p in range(ROWS):
                h = 2 * p - 1 + b
                if h < 0:
                    piece = jnp.zeros((COLS, IN), BF)
                else:
                    piece = wide[layer, h, pl.ds(PAD - 1 + c, COLS, stride=2), :].astype(BF)
                patches[p * COLS : (p + 1) * COLS, lanes] = piece


def own_kernel(low_ref, high_ref, weight_hbm, patches, pre_ref, weight_ref, wide, sem):
    copy = pltpu.make_async_copy(weight_hbm, weight_ref, sem)
    copy.start()
    for layer, source in enumerate((low_ref, high_ref)):
        for h in range(2 * ROWS):
            widen(wide, layer, h, source[h])
        fill_patches(wide, layer, patches, 9 * layer)
    copy.wait()
    pre_ref[...] = jnp.dot(patches[...], weight_ref[9 * IN :, :], preferred_element_type=F32)


def own_taps(low, high, weights):
    return pl.pallas_call(
        own_kernel,
        out_shape=(
            jax.ShapeDtypeStruct((CELLS, 18 * IN), BF),
            jax.ShapeDtypeStruct((CELLS, OUT), F32),
            jax.ShapeDtypeStruct((27 * IN, OUT), BF),
        ),
        in_specs=[VMEM] * 2 + [pl.BlockSpec(memory_space=pltpu.HBM)],
        out_specs=(VMEM,) * 3,
        scratch_shapes=[
            pltpu.VMEM((2, 2 * ROWS, PAD + 2 * COLS, IN), F32),
            pltpu.SemaphoreType.DMA(()),
        ],
        cost_estimate=pl.CostEstimate(flops=2 * CELLS * 18 * IN * OUT, bytes_accessed=3 << 20, transcendentals=0),
        compiler_params=pltpu.CompilerParams(vmem_limit_bytes=GRANT),
        name="own_taps",
    )(low, high, weights)


def weight_terms(patches, first, tap, grad, keep_ref, send_ref):
    lanes = slice((tap - first) * IN, (tap - first + 1) * IN)
    part = lax.dot_general(
        patches[:, lanes], grad, (((0,), (0,)), ((), ())), preferred_element_type=F32
    ).astype(BF)
    for k in range(IN // 16):
        slab, inner = divmod(tap * (IN // 16) + k, SHARE // 16)
        zl, x = divmod(slab, X)
        for half, ref in enumerate((keep_ref, send_ref)):
            ref[x * ZP + zl % ZP, zl // ZP, inner * 16 : (inner + 1) * 16, :] = part[
                k * 16 : (k + 1) * 16, half * HALF : (half + 1) * HALF
            ]


def forward_kernel(
    me_ref, below_ref, weight_ref, own_patches, pre_ref, cot_ref, act_ref, grad_ref, keep_ref, send_ref, patches, wide
):
    for h in range(2 * ROWS):
        widen(wide, 0, h, below_ref[h])
    fill_patches(wide, 0, patches, 0)
    pre = pre_ref[...] + jnp.dot(patches[...], weight_ref[: 9 * IN, :], preferred_element_type=F32)
    sig = jax.nn.sigmoid(pre)
    act_ref[...] = (0.3 * pre + 0.7 * pre * sig).astype(BF)
    slope = 0.3 + 0.7 * (sig + pre * sig * (1.0 - sig))
    grad = (cot_ref[...].astype(F32) * slope).astype(BF)
    grad_ref[...] = grad
    me = me_ref[0]
    place = lax.broadcasted_iota(jnp.int32, (OUT, OUT), 1)
    origin = lax.broadcasted_iota(jnp.int32, (OUT, OUT), 0)
    who = jnp.where(place < HALF, me, 1 - me)
    wanted = (place % HALF) // 8 * 16 + who * 8 + place % 8
    choose = jnp.where(origin == wanted, 1.0, 0.0).astype(BF)
    ordered = jnp.dot(grad, choose, preferred_element_type=F32).astype(BF)
    for tap in range(27):
        held, first = (patches, 0) if tap < 9 else (own_patches, 9)
        weight_terms(held, first, tap, ordered, keep_ref, send_ref)


def forward(me, below, weights, own_patches, pre, cotangent):
    return pl.pallas_call(
        forward_kernel,
        out_shape=(
            jax.ShapeDtypeStruct((CELLS, OUT), BF),
            jax.ShapeDtypeStruct((CELLS, OUT), BF),
            jax.ShapeDtypeStruct((X * ZP, ZQ, SHARE, HALF), BF),
            jax.ShapeDtypeStruct((X * ZP, ZQ, SHARE, HALF), BF),
        ),
        in_specs=[pl.BlockSpec(memory_space=pltpu.SMEM)] + [VMEM] * 5,
        out_specs=(VMEM,) * 4,
        scratch_shapes=[
            pltpu.VMEM((CELLS, 9 * IN), BF),
            pltpu.VMEM((1, 2 * ROWS, PAD + 2 * COLS, IN), F32),
        ],
        cost_estimate=pl.CostEstimate(flops=3 * CELLS * 27 * IN * OUT, bytes_accessed=3 << 20, transcendentals=CELLS * OUT),
        compiler_params=pltpu.CompilerParams(vmem_limit_bytes=GRANT),
        name="forward",
    )(me, below, weights, own_patches, pre, cotangent)


def backward_kernel(grad_ref, next_ref, weight_ref, out_ref, wide):
    def moved(ref):
        grad = ref[...].astype(F32)
        cell = lax.broadcasted_iota(jnp.int32, (CELLS, OUT), 0)
        ahead = jnp.concatenate([grad[1:], jnp.zeros((1, OUT), F32)], axis=0)
        ahead = jnp.where(cell % COLS == COLS - 1, 0.0, ahead)
        blank = jnp.zeros((COLS, OUT), BF)
        found = {}
        for dq, value in ((0, ref[...]), (1, ahead.astype(BF))):
            found[0, dq] = value
            found[1, dq] = jnp.concatenate([value[COLS:], blank], axis=0)
        return found

    mine, after = moved(grad_ref), moved(next_ref)
    choices = {0: [(1, 0)], 1: [(2, 0), (0, 1)]}
    for layer in range(2):
        sources = [(1, mine)] if layer == 0 else [(2, mine), (0, after)]
        for hp in range(2):
            for wp in range(2):
                value = jnp.zeros((CELLS, IN), F32)
                for a, found in sources:
                    for b, dp in choices[hp]:
                        for c, dq in choices[wp]:
                            value += lax.dot_general(
                                found[dp, dq],
                                weight_ref[(a * 3 + b) * 3 + c],
                                (((1,), (1,)), ((), ())),
                                preferred_element_type=F32,
                            )
                for p in range(ROWS):
                    wide[layer, 2 * p + hp, pl.ds(wp, COLS, stride=2), :] = value[p * COLS : (p + 1) * COLS]
    out_ref[...] = wide[...].astype(BF)


def backward(grad, grad_next, weights):
    return pl.pallas_call(
        backward_kernel,
        out_shape=jax.ShapeDtypeStruct((2, 2 * ROWS, 2 * COLS, IN), BF),
        in_specs=[VMEM] * 3,
        out_specs=VMEM,
        scratch_shapes=[pltpu.VMEM((2, 2 * ROWS, 2 * COLS, IN), F32)],
        cost_estimate=pl.CostEstimate(flops=2 * CELLS * 27 * IN * OUT, bytes_accessed=3 << 20, transcendentals=0),
        compiler_params=pltpu.CompilerParams(vmem_limit_bytes=GRANT),
        name="backward",
    )(grad, grad_next, weights)


def exchange(block, axes):
    return lax.all_to_all(block, axes, 0, 0, tiled=True)


def total(parts):
    return jnp.sum(parts.astype(F32), axis=0)


def local(volumes, kernel, cotangent):
    low, high = volumes[0, 0], volumes[0, 1]
    below = shifted(high, 1)
    own_patches, pre, weights = own_taps(low, high, kernel.reshape(27 * IN, OUT))
    me = lax.axis_index("core").reshape(1)
    activation, out_grad, keep, send = forward(
        me, below, weights, own_patches, pre, cotangent.reshape(CELLS, OUT)
    )
    partner = lax.ppermute(send, "core", [(0, 1), (1, 0)])
    grad = (keep.astype(F32) + partner.astype(F32)).astype(BF)
    grad = exchange(grad, ("x", "zp"))
    grad, out_grad = lax.optimization_barrier((grad, out_grad))
    next_grad = shifted(out_grad, -1)
    input_grad = backward(out_grad, next_grad, weights.reshape(27, IN, OUT))
    grad = total(grad).astype(BF)
    grad = grad.reshape(ZQ, SHARE, Y * ZH, 8).transpose(2, 0, 3, 1).reshape(Y * ZH * ZQ, 2, 4 * SHARE)
    grad = total(exchange(grad, ("y", "zh", "zq"))).reshape(8, SHARE).T
    norm_factor = 1.0 / math.sqrt(Y * ZH * CORE * ZL * X * CELLS)
    return (
        activation.reshape(1, 1, ROWS, COLS, OUT),
        input_grad[None],
        grad * norm_factor,
    )


def solution(mesh):
    fine = Mesh(mesh.devices.reshape(Y, ZH, CORE, ZQ, ZP, X), AXES)
    split = P(("y", "zh", "core"), SLAB, None, None, None)
    out_specs = (split, split, P(SLAB, ("y", "zh", "core")))
    return jax.shard_map(local, mesh=fine, in_specs=(split, P(), split), out_specs=out_specs, check_vma=False)
```
